32 devices in a mesh: dp: 4 (over y, x), ctx: 2 (over core), tp: 4 (over z).
Axes of the slice: x: 2, y: 2, z: 4, core: 2. Of those that a mesh axis runs over, the one named last changes fastest.
Arguments:
- tokens: bfloat16 [4, 1024, 4096], P('dp', ('ctx', 'tp')), may hold values from -6 to 6
- norm_gain: float32 [4096], replicated, may hold values from 0.1 to 1.9
- w_qkv: bfloat16 [4096, 3, 4096], P(None, None, 'tp'), may hold values from -8 to 8, as said below
- sub_gain: float32 [4096], P('tp'), may hold values from 0.1 to 1.9
- w_out: bfloat16 [4096, 4096], P('tp'), may hold values from -8 to 8, as said below
Outputs:
- block_out: bfloat16 [4, 1024, 4096], P('dp', ('ctx', 'tp'))
The draws below stay inside these ranges and needn't reach their ends.
Inputs may be any that keep to these rules, and one draw needn't show every extreme that they name: For each m, no entry of w_qkv[:, m, :] has a magnitude between 0.35 and 3 times half the mean magnitude of w_qkv[:, m, :]. No entry of w_out has a magnitude between 0.35 and 3 times half the mean magnitude of w_out.
All inputs are finite; a program needn't handle non-finite values.
Results may differ from the reference program's by a relative error of at most 0.012.
Values may be sent and summed in bfloat16 or wider, within the bound.
A program may use at most 192 MiB of HBM per device.

```python
import jax
import jax.numpy as jnp
from jax import lax

D = 4096
H = 32
HD = 128
B = 4
S = 1024
N_TP = 4


def banded(key, shape, density):
    keys = jax.random.split(key, 4)
    alive = jax.random.uniform(keys[0], shape, jnp.float32) < density
    large = jax.random.uniform(keys[1], shape, jnp.float32, 0.5, 1.5)
    little = jax.random.uniform(keys[2], shape, jnp.float32, 0.0, 0.01)
    signs = jnp.where(jax.random.bernoulli(keys[3], 0.5, shape), 1.0, -1.0)
    return signs * jnp.where(alive, large, little)


def draw_tokens(key, part):
    keys = jax.random.split(key, 1)
    return jnp.clip(jax.random.normal(keys[0], (B, S, D), jnp.float32), -6.0, 6.0).astype(jnp.bfloat16)


def draw_w_qkv(key, part):
    width = H * HD
    keys = jax.random.split(key, 3)
    place = jnp.arange(width, dtype=jnp.float32) / (width - 1)
    spread = jnp.power(10.0, -0.7 * jax.random.uniform(keys[1], (width,), jnp.float32))
    row_density = jnp.power(10.0, -jax.random.uniform(keys[2], (D, 3, 1), jnp.float32))
    rise = jnp.power(3.0, place - 1.0)
    density = row_density * (rise * spread)[None, None, :]
    full = banded(keys[0], (D, 3, width), density)
    return (full * (24.0 / jnp.sqrt(jnp.float32(D)))).astype(jnp.bfloat16)


def draw_w_out(key, part):
    width = H * HD
    keys = jax.random.split(key, 3)
    place = jnp.arange(width, dtype=jnp.float32) / (width - 1)
    spread = jnp.power(10.0, -0.7 * jax.random.uniform(keys[1], (width,), jnp.float32))
    col_density = jnp.power(10.0, -jax.random.uniform(keys[2], (D,), jnp.float32))
    rise = jnp.power(3.0, place - 1.0)
    density = (rise * spread)[:, None] * col_density[None, :]
    return (banded(keys[0], (width, D), density) * (24.0 / jnp.sqrt(jnp.float32(width)))).astype(jnp.bfloat16)


def setup_inputs(seed: int = 0) -> dict:
    splits = jax.random.split(jax.random.key(seed), 6)
    return {
        "tokens": draw_tokens(jax.random.fold_in(splits[5], 71), 0),
        "norm_gain": jnp.clip(1.0 + 0.18 * jax.random.normal(splits[1], (D,), jnp.float32), 0.1, 1.9),
        "w_qkv": draw_w_qkv(jax.random.fold_in(splits[5], 71), 0),
        "sub_gain": jnp.clip(1.0 + 0.18 * jax.random.normal(splits[3], (H * HD,), jnp.float32), 0.1, 1.9),
        "w_out": draw_w_out(jax.random.fold_in(splits[5], 71), 0),
    }


eps_norm = 1e-05

def quantize(weight, scale):
    ratio = weight.astype(jnp.float32) / scale
    ternary = jnp.where(ratio > 0.5, 1.0, jnp.where(ratio < -0.5, -1.0, 0.0))
    return (scale * ternary).astype(jnp.bfloat16)

def reference(tokens, norm_gain, w_qkv, sub_gain, w_out):
    count = float(D * H * HD)
    width = H * HD
    qkv_scale = lax.optimization_barrier(jnp.sum(jnp.abs(w_qkv.astype(jnp.float32)), axis=(0, 2))) / count
    w_in = quantize(w_qkv, qkv_scale[None, :, None])
    out_scale = jnp.sum(jnp.abs(w_out.astype(jnp.float32))) / count
    w_o = quantize(w_out, out_scale)
    w_blocks = w_o.reshape(N_TP, width // N_TP, D)
    inv_root = 1.0 / jnp.sqrt(jnp.float32(HD))
    positions = jnp.arange(S)
    causal = positions[None, :] <= positions[:, None]

    def one_seq(seq):
        inputs = seq.astype(jnp.float32)
        normed = (inputs * lax.rsqrt(lax.optimization_barrier(jnp.mean(inputs * inputs, axis=-1, keepdims=True)) + eps_norm) * norm_gain).astype(jnp.bfloat16)
        query = jnp.dot(normed, w_in[:, 0, :], preferred_element_type=jnp.float32).astype(jnp.bfloat16)
        keys = jnp.dot(normed, w_in[:, 1, :], preferred_element_type=jnp.float32).astype(jnp.bfloat16)
        values = jnp.dot(normed, w_in[:, 2, :], preferred_element_type=jnp.float32).astype(jnp.bfloat16)
        q_heads = query.reshape(S, H, HD).transpose(1, 0, 2)
        k_heads = keys.reshape(S, H, HD).transpose(1, 0, 2)
        v_heads = values.reshape(S, H, HD).transpose(1, 0, 2)

        def one_head(triple):
            q_one, k_one, v_one = triple
            score = jnp.dot(q_one, k_one.T, preferred_element_type=jnp.float32) * inv_root
            score = jnp.where(causal, score, -jnp.inf)
            top = lax.optimization_barrier(jnp.max(score, axis=-1, keepdims=True))
            expo = jnp.where(causal, jnp.exp(score - top), 0.0)
            total = lax.optimization_barrier(jnp.sum(expo, axis=-1, keepdims=True))
            return jnp.dot(expo.astype(jnp.bfloat16), v_one, preferred_element_type=jnp.float32) / total
        attended = lax.map(one_head, (q_heads, k_heads, v_heads))
        attended = attended.transpose(1, 0, 2).reshape(S, width)
        power = lax.optimization_barrier(jnp.mean(attended * attended, axis=-1, keepdims=True))
        sub_normed = (attended * lax.rsqrt(power + eps_norm) * sub_gain).astype(jnp.bfloat16)
        parts = sub_normed.reshape(S, N_TP, width // N_TP).transpose(1, 0, 2)

        def add_block(total, pair):
            part, w_part = pair
            term = jnp.dot(part, w_part, preferred_element_type=jnp.float32).astype(jnp.bfloat16)
            return (total + term.astype(jnp.float32), None)
        projected, _ = lax.scan(add_block, jnp.zeros((S, D), jnp.float32), (parts, w_blocks))
        return (inputs + projected).astype(jnp.bfloat16)
    return lax.map(one_seq, tokens)
```

```python
import functools

import jax
import jax.numpy as jnp
from jax import lax
from jax.experimental import pallas as pl
from jax.experimental.pallas import tpu as pltpu
from jax.sharding import PartitionSpec as P

HD = 128
eps_norm = 1e-05
low_value = -1e30
MESH = pl.DeviceIdType.MESH
F32 = jnp.float32
BF16 = jnp.bfloat16
VMEM_LIMIT = 60 * 1024 * 1024


def mult(x, k):
    return pl.multiple_of(x, k)


def enter(n, c, z):
    barrier = pltpu.get_barrier_semaphore()
    flat = c * n + z

    def greet(j, carry):
        other = lax.rem(flat + j, 2 * n)
        pl.semaphore_signal(
            barrier,
            inc=1,
            device_id={"ctx": other // n, "tp": lax.rem(other, n)},
            device_id_type=MESH,
        )
        return carry

    lax.fori_loop(1, 2 * n, greet, 0)
    pl.semaphore_wait(barrier, 2 * n - 1)


def tile_copy(n, c, z, src, dst, send_sem, recv_sem, j):
    flat = c * n + z
    other = lax.rem(flat + j, 2 * n)
    return pltpu.make_async_remote_copy(
        src_ref=src,
        dst_ref=dst.at[flat],
        send_sem=send_sem.at[other],
        recv_sem=recv_sem.at[flat],
        device_id={"ctx": other // n, "tp": lax.rem(other, n)},
        device_id_type=MESH,
    )


def tile_wait(n, c, z, src, dst, send_sem, recv_sem, j):
    flat = c * n + z
    other = lax.rem(flat + j, 2 * n)
    return pltpu.make_async_remote_copy(
        src_ref=src,
        dst_ref=dst.at[other],
        send_sem=send_sem.at[other],
        recv_sem=recv_sem.at[other],
        device_id={"ctx": other // n, "tp": lax.rem(other, n)},
        device_id_type=MESH,
    )


def project_kernel(
    n, count, pieces,
    x_ref, gain_ref, w_ref, wo_ref,
    qkv_ref, wo_out, scale_ref,
    held, w_held, wo_held, part, sums,
    load_sem, store_sem, tile_send, tile_recv, send_r, send_l, send_p, recv_z, recv_p,
):
    c = lax.axis_index("ctx")
    z = lax.axis_index("tp")
    rows, width = x_ref.shape
    cols = w_held.shape[2]
    deep = width // pieces
    deep_o = wo_held.shape[0] // pieces

    def load_w(m, p):
        return pltpu.make_async_copy(
            w_ref.at[m, pl.ds(p * deep, deep), pl.ds(mult(c * cols, 128), cols)],
            w_held.at[m, pl.ds(p * deep, deep)],
            load_sem.at[m * pieces + p],
        )

    def load_o(p):
        return pltpu.make_async_copy(
            wo_ref.at[pl.ds(p * deep_o, deep_o)],
            wo_held.at[pl.ds(p * deep_o, deep_o)],
            load_sem.at[3 * pieces + p],
        )

    for m in range(3):
        for p in range(pieces):
            load_w(m, p).start()
    for p in range(pieces):
        load_o(p).start()

    mine = mult(c * rows, 16)

    def norm_rows(i, carry):
        x = x_ref[pl.ds(mult(i * 16, 16), 16), :].astype(F32)
        r = lax.rsqrt(jnp.mean(x * x, axis=-1, keepdims=True) + eps_norm)
        held[z, pl.ds(mult(mine + i * 16, 16), 16), :] = (x * r * gain_ref[...]).astype(BF16)
        return carry

    lax.fori_loop(0, rows // 16, norm_rows, 0)
    enter(n, c, z)

    def move(owner, to, send_sem, recv_sem):
        block = held.at[owner, pl.ds(mine, rows)]
        return pltpu.make_async_remote_copy(
            src_ref=block,
            dst_ref=block,
            send_sem=send_sem.at[owner],
            recv_sem=recv_sem.at[owner],
            device_id=to,
            device_id_type=MESH,
        )

    def to_right(owner):
        return move(owner, {"tp": lax.rem(z + 1, n)}, send_r, recv_z)

    def to_left(owner):
        return move(owner, {"tp": lax.rem(z + n - 1, n)}, send_l, recv_z)

    def to_partner(owner):
        return move(owner, {"ctx": 1 - c}, send_p, recv_p)

    def from_partner(owner):
        block = held.at[owner, pl.ds(mult((1 - c) * rows, 16), rows)]
        return pltpu.make_async_remote_copy(
            src_ref=block,
            dst_ref=block,
            send_sem=send_p.at[owner],
            recv_sem=recv_p.at[owner],
            device_id={"ctx": 1 - c},
            device_id_type=MESH,
        )

    @pl.when(z < n - 1)
    def _():
        to_right(z).start()

    @pl.when(z > 0)
    def _():
        to_left(z).start()

    to_partner(z).start()

    part[...] = jnp.zeros_like(part)
    step_w = 32
    for m in range(3):
        total = jnp.zeros((8, cols), F32)
        for p in range(pieces):
            load_w(m, p).wait()

            def add_w(i, acc, m=m, p=p):
                at = mult(p * deep + i * step_w, step_w)
                v = jnp.abs(w_held[m, pl.ds(at, step_w), :].astype(F32))
                return acc + jnp.sum(v.reshape(step_w // 8, 8, cols), axis=0)

            total = lax.fori_loop(0, deep // step_w, add_w, total)
        one = jnp.sum(jnp.sum(total, axis=0, keepdims=True), axis=1, keepdims=True)
        part[m : m + 1, :] = jnp.broadcast_to(one, (1, 128))
    total = jnp.zeros((8, width), F32)
    for p in range(pieces):
        load_o(p).wait()

        def add_o(i, acc, p=p):
            v = jnp.abs(wo_held[pl.ds(mult(p * deep_o + i * 16, 16), 16), :].astype(F32))
            return acc + jnp.sum(v.reshape(2, 8, width), axis=0)

        total = lax.fori_loop(0, deep_o // 16, add_o, total)
    one = 0.5 * jnp.sum(jnp.sum(total, axis=0, keepdims=True), axis=1, keepdims=True)
    part[3:4, :] = jnp.broadcast_to(one, (1, 128))

    def send_tile(j, carry):
        tile_copy(n, c, z, part, sums, tile_send, tile_recv, j).start()
        return carry

    lax.fori_loop(1, 2 * n, send_tile, 0)

    def get_tile(j, acc):
        tile_wait(n, c, z, part, sums, tile_send, tile_recv, j).wait_recv()
        return acc + sums[lax.rem(c * n + z + j, 2 * n)]

    scale = lax.fori_loop(1, 2 * n, get_tile, part[...]) / count
    scale_ref[...] = scale

    def ternary(w, half):
        one = jnp.ones_like(w)
        zero = jnp.zeros_like(w)
        return jnp.where(w > half, one, jnp.where(w < -half, -one, zero))

    for m in range(3):
        half_w = jnp.broadcast_to((0.5 * scale[m : m + 1, 0:1]).astype(BF16), (step_w, cols))

        def cut_w(i, carry, m=m, half_w=half_w):
            at = pl.ds(mult(i * step_w, step_w), step_w)
            w_held[m, at, :] = ternary(w_held[m, at, :], half_w)
            return carry

        lax.fori_loop(0, width // step_w, cut_w, 0)

    block_rows = n * rows

    def compute(owner):
        from_partner(owner).wait_recv()

        def one(m, carry):
            s = scale_ref[pl.ds(m, 1), 0:1].astype(BF16).astype(F32)
            y = jnp.dot(held[owner], w_held[m], preferred_element_type=F32) * s
            y = y.astype(BF16)
            qkv_ref[m, pl.ds(mult(owner * rows, 16), rows), :] = y[:rows]
            qkv_ref[m, pl.ds(mult(block_rows + owner * rows, 16), rows), :] = y[rows:]
            return carry

        lax.fori_loop(0, 3, one, 0)

    def forward(s):
        @pl.when(z - 1 - s >= 0)
        def _():
            owner = lax.rem(z - 1 - s + n, n)
            to_right(owner).wait_recv()

            @pl.when(z < n - 1)
            def _():
                to_right(owner).start()

            to_partner(owner).start()

        @pl.when(z + 1 + s <= n - 1)
        def _():
            owner = lax.rem(z + 1 + s, n)
            to_left(owner).wait_recv()

            @pl.when(z > 0)
            def _():
                to_left(owner).start()

            to_partner(owner).start()

    def store_o():
        return pltpu.make_async_copy(wo_held, wo_out, store_sem)

    compute(z)
    half_o = jnp.broadcast_to((0.5 * scale[3:4, 0:1]).astype(BF16), (16, width))

    def cut_o(i, carry):
        at = pl.ds(mult(i * 16, 16), 16)
        wo_held[at, :] = ternary(wo_held[at, :], half_o)
        return carry

    forward(0)
    lax.fori_loop(0, wo_held.shape[0] // 16, cut_o, 0)
    store_o().start()

    def step(s, carry):
        @pl.when(s < n - 1)
        def _():
            forward(s)

        @pl.when(z - s >= 0)
        def _():
            compute(lax.rem(z - s + n, n))

        @pl.when(z + s <= n - 1)
        def _():
            compute(lax.rem(z + s, n))

        return carry

    lax.fori_loop(1, n, step, 0)

    def finish(owner, carry):
        @pl.when((owner <= z) & (z < n - 1))
        def _():
            to_right(owner).wait_send()

        @pl.when((owner >= z) & (z > 0))
        def _():
            to_left(owner).wait_send()

        to_partner(owner).wait_send()
        return carry

    lax.fori_loop(0, n, finish, 0)

    def finish_tile(j, carry):
        tile_wait(n, c, z, part, sums, tile_send, tile_recv, j).wait_send()
        return carry

    lax.fori_loop(1, 2 * n, finish_tile, 0)
    store_o().wait()


def attend_kernel(block, qkv_ref, gain_ref, out_ref, power_ref):
    rows = qkv_ref.shape[1]
    factor = (HD**-0.5) * 1.4426950408889634
    lower = lax.broadcasted_iota(jnp.int32, (block, block), 1) <= lax.broadcasted_iota(
        jnp.int32, (block, block), 0
    )
    turn = (((1,), (1,)), ((), ()))

    @pl.when(pl.program_id(0) == 0)
    def _():
        power_ref[...] = jnp.zeros_like(power_ref)

    for i in range(rows // block):
        here = slice(i * block, (i + 1) * block)
        q = qkv_ref[0, here, :]
        diag = lax.dot_general(q, qkv_ref[1, here, :], turn, preferred_element_type=F32)
        diag = jnp.where(lower, diag, low_value)
        top = jnp.max(diag, axis=-1, keepdims=True)
        if i:
            past = slice(0, i * block)
            back = lax.dot_general(q, qkv_ref[1, past, :], turn, preferred_element_type=F32)
            top = jnp.maximum(top, jnp.max(back, axis=-1, keepdims=True))
        e = jnp.exp2((diag - top) * factor)
        total = jnp.sum(e, axis=-1, keepdims=True)
        acc = jnp.dot(e.astype(BF16), qkv_ref[2, here, :], preferred_element_type=F32)
        if i:
            e = jnp.exp2((back - top) * factor)
            total = total + jnp.sum(e, axis=-1, keepdims=True)
            acc = acc + jnp.dot(e.astype(BF16), qkv_ref[2, past, :], preferred_element_type=F32)
        att = acc / total
        power_ref[here, :] += att * att
        out_ref[here, :] = (att * gain_ref[...]).astype(BF16)


def scatter_kernel(
    n, width_all,
    a_ref, power_ref, wo_ref, scale_ref, x_ref,
    out_ref,
    a_held, wo_held, mine_p, got, extra, tiles, sums,
    load_sem, keep_sem, pair_send, pair_recv, tile_send, tile_recv, send_sem, recv_sem, extra_sem,
):
    c = lax.axis_index("ctx")
    z = lax.axis_index("tp")
    rows, width = x_ref.shape
    cols = a_ref.shape[1]
    block_rows = n * rows
    load = pltpu.make_async_copy(wo_ref, wo_held, load_sem)
    load.start()
    mine = pl.ds(mult(c * block_rows, 16), block_rows)
    theirs = pl.ds(mult((1 - c) * block_rows, 16), block_rows)
    keep = pltpu.make_async_copy(a_ref.at[mine], a_held.at[c], keep_sem)
    keep.start()

    def sum_tile(b, carry):
        ones = jnp.ones((8, 128), F32)
        blk = power_ref[pl.ds(mult(b * rows, 8), rows), :]
        tiles[b] = lax.dot_general(
            ones, blk, (((1,), (1,)), ((), ())),
            precision=lax.Precision.HIGHEST, preferred_element_type=F32,
        )
        return carry

    lax.fori_loop(0, 2 * n, sum_tile, 0)
    enter(n, c, z)
    swap = pltpu.make_async_remote_copy(
        src_ref=a_ref.at[theirs],
        dst_ref=a_held.at[c],
        send_sem=pair_send,
        recv_sem=pair_recv,
        device_id={"ctx": 1 - c},
        device_id_type=MESH,
    )
    swap.start()

    def send_tile(j, carry):
        other = lax.rem(c * n + z + j, 2 * n)
        tile_copy(n, c, z, tiles.at[other], sums, tile_send, tile_recv, j).start()
        return carry

    lax.fori_loop(1, 2 * n, send_tile, 0)
    keep.wait()
    load.wait()
    swap.wait_recv()

    left = {"tp": lax.rem(z + n - 1, n)}
    right = {"tp": lax.rem(z + 1, n)}

    def move(t, dst, recv, to):
        return pltpu.make_async_remote_copy(
            src_ref=mine_p.at[t],
            dst_ref=dst,
            send_sem=send_sem.at[t],
            recv_sem=recv,
            device_id=to,
            device_id_type=MESH,
        )

    def to_left(t):
        return move(t, got.at[t], recv_sem.at[t], left)

    def to_right_pass(t):
        return move(t, got.at[t], recv_sem.at[t], right)

    def to_right_last(t):
        return move(t, extra, extra_sem, right)

    def start_right(t):
        @pl.when(t == z + 1)
        def _():
            to_right_last(t).start()

        @pl.when(t > z + 1)
        def _():
            to_right_pass(t).start()

    tn = min(512, width)
    scale_o = scale_ref[3:4, 0:1].astype(BF16).astype(F32)

    def target(i):
        return lax.select(2 * z >= n, i, n - 1 - i)

    def first(i, carry):
        t = target(i)
        at = pl.ds(mult(t * rows, 16), rows)

        def cols_of(k, inner):
            there = pl.ds(mult(k * tn, 128), tn)
            y = jnp.dot(a_held[0, at, :], wo_held[:cols, there], preferred_element_type=F32)
            y = y + jnp.dot(a_held[1, at, :], wo_held[cols:, there], preferred_element_type=F32)
            mine_p[t, :, there] = (y * scale_o).astype(BF16)
            return inner

        lax.fori_loop(0, width // tn, cols_of, 0)

        @pl.when((z == n - 1) & (t < z))
        def _():
            to_left(t).start()

        @pl.when((z == 0) & (t > z))
        def _():
            start_right(t)

        return carry

    lax.fori_loop(0, n, first, 0)

    def add_got(t):
        def some(i, inner):
            at = pl.ds(mult(i * 16, 16), 16)
            mine_p[t, at, :] = (
                mine_p[t, at, :].astype(F32) + got[t, at, :].astype(F32)
            ).astype(BF16)
            return inner

        lax.fori_loop(0, rows // 16, some, 0)

    def pass_left(t):
        @pl.when((t < z) & (z < n - 1))
        def _():
            to_left(t).wait_recv()
            add_got(t)
            to_left(t).start()

    def pass_right(t):
        @pl.when((t > z) & (z > 0))
        def _():
            to_right_pass(t).wait_recv()
            add_got(t)
            start_right(t)

    def second(i, carry):
        @pl.when(2 * z >= n)
        def _():
            pass_left(i)

        pass_right(n - 1 - i)

        @pl.when(2 * z < n)
        def _():
            pass_left(i)

        return carry

    lax.fori_loop(0, n, second, 0)

    def get_tile(j, acc):
        tile_wait(n, c, z, tiles.at[0], sums, tile_send, tile_recv, j).wait_recv()
        return acc + sums[lax.rem(c * n + z + j, 2 * n)]

    power = lax.fori_loop(1, 2 * n, get_tile, tiles[c * n + z]) / width_all
    r = lax.rsqrt(power[0:1, :] + eps_norm)
    r_col = jnp.transpose(jnp.broadcast_to(r, (rows, rows)))
    tiles_of = width // rows
    sums_r = r_col

    @pl.when(z < n - 1)
    def _():
        to_left(z).wait_recv()

    @pl.when(z > 0)
    def _():
        to_right_last(z).wait_recv()

    @pl.when(z == n - 1)
    def _():
        got[z] = jnp.zeros((rows, width), BF16)

    @pl.when(z == 0)
    def _():
        extra[...] = jnp.zeros((rows, width), BF16)

    def last(k, carry):
        at = pl.ds(mult(k * rows, 128), rows)
        y = mine_p[z, :, at].astype(F32) + got[z, :, at].astype(F32) + extra[:, at].astype(F32)
        out_ref[:, at] = (x_ref[:, at].astype(F32) + y * sums_r).astype(BF16)
        return carry

    lax.fori_loop(0, tiles_of, last, 0)

    def finish(t, carry):
        @pl.when(t < z)
        def _():
            to_left(t).wait_send()

        @pl.when(t > z)
        def _():
            to_right_pass(t).wait_send()

        return carry

    lax.fori_loop(0, n, finish, 0)

    def finish_tile(j, carry):
        tile_wait(n, c, z, tiles.at[0], sums, tile_send, tile_recv, j).wait_send()
        return carry

    lax.fori_loop(1, 2 * n, finish_tile, 0)
    swap.wait_send()


def body(n, tokens, norm_gain, w_qkv, sub_gain, w_out):
    x = tokens[0]
    rows, width = x.shape
    head_cols = w_qkv.shape[2]
    cols = head_cols // 2
    heads = cols // HD
    all_rows = 2 * n * rows
    count = float(width * n * head_cols)
    pieces = 4
    w = jnp.transpose(w_qkv, (1, 0, 2))
    dma = pltpu.SemaphoreType.DMA
    vm = pl.BlockSpec(memory_space=pltpu.VMEM)
    hbm = pl.BlockSpec(memory_space=pl.ANY)
    qkv, wo, scale = pl.pallas_call(
        functools.partial(project_kernel, n, count, pieces),
        out_shape=(
            jax.ShapeDtypeStruct((3, all_rows, cols), BF16),
            jax.ShapeDtypeStruct(w_out.shape, BF16),
            jax.ShapeDtypeStruct((8, 128), F32),
        ),
        in_specs=[vm, vm, hbm, hbm],
        out_specs=(vm, hbm, vm),
        scratch_shapes=[
            pltpu.VMEM((n, 2 * rows, width), BF16),
            pltpu.VMEM((3, width, cols), BF16),
            pltpu.VMEM(w_out.shape, BF16),
            pltpu.VMEM((8, 128), F32),
            pltpu.VMEM((2 * n, 8, 128), F32),
            dma((4 * pieces,)),
            dma(()),
            dma((2 * n,)),
            dma((2 * n,)),
            dma((n,)),
            dma((n,)),
            dma((n,)),
            dma((n,)),
            dma((n,)),
        ],
        compiler_params=pltpu.CompilerParams(
            collective_id=0, has_side_effects=True, vmem_limit_bytes=VMEM_LIMIT
        ),
        name="project",
    )(x, norm_gain.reshape(1, width), w, w_out)

    gain = lax.dynamic_slice(sub_gain, (lax.axis_index("ctx") * cols,), (cols,)).reshape(1, cols)
    att, power = pl.pallas_call(
        functools.partial(attend_kernel, 256),
        grid=(heads,),
        out_shape=(
            jax.ShapeDtypeStruct((all_rows, cols), BF16),
            jax.ShapeDtypeStruct((all_rows, HD), F32),
        ),
        in_specs=[
            pl.BlockSpec((3, all_rows, HD), lambda h: (0, 0, h)),
            pl.BlockSpec((1, HD), lambda h: (0, h)),
        ],
        out_specs=(
            pl.BlockSpec((all_rows, HD), lambda h: (0, h)),
            pl.BlockSpec((all_rows, HD), lambda h: (0, 0)),
        ),
        compiler_params=pltpu.CompilerParams(
            dimension_semantics=("arbitrary",), vmem_limit_bytes=VMEM_LIMIT
        ),
        name="attend",
    )(qkv, gain)

    out = pl.pallas_call(
        functools.partial(scatter_kernel, n, float(n * head_cols)),
        out_shape=jax.ShapeDtypeStruct((rows, width), BF16),
        in_specs=[vm, vm, hbm, vm, vm],
        out_specs=vm,
        scratch_shapes=[
            pltpu.VMEM((2, n * rows, cols), BF16),
            pltpu.VMEM(w_out.shape, BF16),
            pltpu.VMEM((n, rows, width), BF16),
            pltpu.VMEM((n, rows, width), BF16),
            pltpu.VMEM((rows, width), BF16),
            pltpu.VMEM((2 * n, 8, 128), F32),
            pltpu.VMEM((2 * n, 8, 128), F32),
            dma(()),
            dma(()),
            dma(()),
            dma(()),
            dma((2 * n,)),
            dma((2 * n,)),
            dma((n,)),
            dma((n,)),
            dma(()),
        ],
        compiler_params=pltpu.CompilerParams(
            collective_id=1, has_side_effects=True, vmem_limit_bytes=VMEM_LIMIT
        ),
        name="scatter",
    )(att, power, wo, scale, x)
    return out[None]


def solution(mesh):
    return jax.shard_map(
        functools.partial(body, mesh.shape["tp"]),
        mesh=mesh,
        in_specs=(P("dp", ("ctx", "tp"), None), P(), P(None, None, "tp"), P("tp"), P("tp", None)),
        out_specs=P("dp", ("ctx", "tp"), None),
        check_vma=False,
    )
```

```python
import functools

import jax
import jax.numpy as jnp
from jax import lax
from jax.experimental import pallas as pl
from jax.experimental.pallas import tpu as pltpu
from jax.sharding import PartitionSpec as P

HD = 128
eps_norm = 1e-05
low_value = -1e30
MESH = pl.DeviceIdType.MESH
F32 = jnp.float32
BF16 = jnp.bfloat16
VMEM_LIMIT = 60 * 1024 * 1024


def mult(x, k):
    return pl.multiple_of(x, k)


def enter(n, c, z):
    barrier = pltpu.get_barrier_semaphore()
    flat = c * n + z

    def greet(j, carry):
        other = lax.rem(flat + j, 2 * n)
        pl.semaphore_signal(
            barrier,
            inc=1,
            device_id={"ctx": other // n, "tp": lax.rem(other, n)},
            device_id_type=MESH,
        )
        return carry

    lax.fori_loop(1, 2 * n, greet, 0)
    pl.semaphore_wait(barrier, 2 * n - 1)


def tile_copy(n, c, z, src, dst, send_sem, recv_sem, j):
    flat = c * n + z
    other = lax.rem(flat + j, 2 * n)
    return pltpu.make_async_remote_copy(
        src_ref=src,
        dst_ref=dst.at[flat],
        send_sem=send_sem.at[other],
        recv_sem=recv_sem.at[flat],
        device_id={"ctx": other // n, "tp": lax.rem(other, n)},
        device_id_type=MESH,
    )


def tile_wait(n, c, z, src, dst, send_sem, recv_sem, j):
    flat = c * n + z
    other = lax.rem(flat + j, 2 * n)
    return pltpu.make_async_remote_copy(
        src_ref=src,
        dst_ref=dst.at[other],
        send_sem=send_sem.at[other],
        recv_sem=recv_sem.at[other],
        device_id={"ctx": other // n, "tp": lax.rem(other, n)},
        device_id_type=MESH,
    )


def layer_kernel(
    n, count, width_all, pieces, block,
    x_ref, gain_ref, w_ref, sub_ref, wo_ref,
    out_ref,
    held, w_held, wo_held, qkv_ref, scale_ref, part, sums,
    a_ref, a_held, power_ref, extra, tiles, psums,
    load_sem, tile_send, tile_recv, send_r, send_l, send_p, recv_z, recv_p,
    free_l, free_r, keep_sem, pair_send, pair_recv, ptile_send, ptile_recv,
    send_sem, recv_sem, extra_sem,
):
    c = lax.axis_index("ctx")
    z = lax.axis_index("tp")
    rows, width = x_ref.shape
    cols = w_held.shape[2]
    deep = width // pieces
    deep_o = wo_held.shape[0] // pieces

    def load_w(m, p):
        return pltpu.make_async_copy(
            w_ref.at[m, pl.ds(p * deep, deep), pl.ds(mult(c * cols, 128), cols)],
            w_held.at[m, pl.ds(p * deep, deep)],
            load_sem.at[m * pieces + p],
        )

    def load_o(p):
        return pltpu.make_async_copy(
            wo_ref.at[pl.ds(p * deep_o, deep_o)],
            wo_held.at[pl.ds(p * deep_o, deep_o)],
            load_sem.at[3 * pieces + p],
        )

    for m in range(3):
        for p in range(pieces):
            load_w(m, p).start()
    for p in range(pieces):
        load_o(p).start()

    mine = mult(c * rows, 16)

    def norm_rows(i, carry):
        x = x_ref[pl.ds(mult(i * 16, 16), 16), :].astype(F32)
        r = lax.rsqrt(jnp.mean(x * x, axis=-1, keepdims=True) + eps_norm)
        held[z, pl.ds(mult(mine + i * 16, 16), 16), :] = (x * r * gain_ref[...]).astype(BF16)
        return carry

    lax.fori_loop(0, rows // 16, norm_rows, 0)
    enter(n, c, z)

    def move(owner, to, send_sem, recv_sem):
        block = held.at[owner, pl.ds(mine, rows)]
        return pltpu.make_async_remote_copy(
            src_ref=block,
            dst_ref=block,
            send_sem=send_sem.at[owner],
            recv_sem=recv_sem.at[owner],
            device_id=to,
            device_id_type=MESH,
        )

    def to_right(owner):
        return move(owner, {"tp": lax.rem(z + 1, n)}, send_r, recv_z)

    def to_left(owner):
        return move(owner, {"tp": lax.rem(z + n - 1, n)}, send_l, recv_z)

    def to_partner(owner):
        return move(owner, {"ctx": 1 - c}, send_p, recv_p)

    def from_partner(owner):
        block = held.at[owner, pl.ds(mult((1 - c) * rows, 16), rows)]
        return pltpu.make_async_remote_copy(
            src_ref=block,
            dst_ref=block,
            send_sem=send_p.at[owner],
            recv_sem=recv_p.at[owner],
            device_id={"ctx": 1 - c},
            device_id_type=MESH,
        )

    @pl.when(z < n - 1)
    def _():
        to_right(z).start()

    @pl.when(z > 0)
    def _():
        to_left(z).start()

    to_partner(z).start()

    part[...] = jnp.zeros_like(part)
    step_w = 32
    for m in range(3):
        total = jnp.zeros((8, cols), F32)
        for p in range(pieces):
            load_w(m, p).wait()

            def add_w(i, acc, m=m, p=p):
                at = mult(p * deep + i * step_w, step_w)
                v = jnp.abs(w_held[m, pl.ds(at, step_w), :].astype(F32))
                return acc + jnp.sum(v.reshape(step_w // 8, 8, cols), axis=0)

            total = lax.fori_loop(0, deep // step_w, add_w, total)
        one = jnp.sum(jnp.sum(total, axis=0, keepdims=True), axis=1, keepdims=True)
        part[m : m + 1, :] = jnp.broadcast_to(one, (1, 128))
    total = jnp.zeros((8, width), F32)
    for p in range(pieces):
        load_o(p).wait()

        def add_o(i, acc, p=p):
            v = jnp.abs(wo_held[pl.ds(mult(p * deep_o + i * 16, 16), 16), :].astype(F32))
            return acc + jnp.sum(v.reshape(2, 8, width), axis=0)

        total = lax.fori_loop(0, deep_o // 16, add_o, total)
    one = 0.5 * jnp.sum(jnp.sum(total, axis=0, keepdims=True), axis=1, keepdims=True)
    part[3:4, :] = jnp.broadcast_to(one, (1, 128))

    def send_tile(j, carry):
        tile_copy(n, c, z, part, sums, tile_send, tile_recv, j).start()
        return carry

    lax.fori_loop(1, 2 * n, send_tile, 0)

    def forward(s):
        @pl.when(z - 1 - s >= 0)
        def _():
            owner = lax.rem(z - 1 - s + n, n)
            to_right(owner).wait_recv()

            @pl.when(z < n - 1)
            def _():
                to_right(owner).start()

            to_partner(owner).start()

        @pl.when(z + 1 + s <= n - 1)
        def _():
            owner = lax.rem(z + 1 + s, n)
            to_left(owner).wait_recv()

            @pl.when(z > 0)
            def _():
                to_left(owner).start()

            to_partner(owner).start()

    forward(0)

    def get_tile(j, acc):
        tile_wait(n, c, z, part, sums, tile_send, tile_recv, j).wait_recv()
        return acc + sums[lax.rem(c * n + z + j, 2 * n)]

    scale = lax.fori_loop(1, 2 * n, get_tile, part[...]) / count
    scale_ref[...] = scale

    def ternary(w, half):
        one = jnp.ones_like(w)
        zero = jnp.zeros_like(w)
        return jnp.where(w > half, one, jnp.where(w < -half, -one, zero))

    for m in range(3):
        half_w = jnp.broadcast_to((0.5 * scale[m : m + 1, 0:1]).astype(BF16), (step_w, cols))

        def cut_w(i, carry, m=m, half_w=half_w):
            at = pl.ds(mult(i * step_w, step_w), step_w)
            w_held[m, at, :] = ternary(w_held[m, at, :], half_w)
            return carry

        lax.fori_loop(0, width // step_w, cut_w, 0)

    block_rows = n * rows

    def compute(owner):
        from_partner(owner).wait_recv()

        def one(m, carry):
            s = scale_ref[pl.ds(m, 1), 0:1].astype(BF16).astype(F32)
            y = jnp.dot(held[owner], w_held[m], preferred_element_type=F32) * s
            y = y.astype(BF16)
            qkv_ref[m, pl.ds(mult(owner * rows, 16), rows), :] = y[:rows]
            qkv_ref[m, pl.ds(mult(block_rows + owner * rows, 16), rows), :] = y[rows:]
            return carry

        lax.fori_loop(0, 3, one, 0)

    compute(z)

    def cut_out():
        half_o = jnp.broadcast_to((0.5 * scale_ref[3:4, 0:1]).astype(BF16), (16, width))

        def cut_o(i, carry):
            at = pl.ds(mult(i * 16, 16), 16)
            wo_held[at, :] = ternary(wo_held[at, :], half_o)
            return carry

        lax.fori_loop(0, wo_held.shape[0] // 16, cut_o, 0)

    def compute_both(s):
        @pl.when(z - 1 - s >= 0)
        def _():
            compute(lax.rem(z - 1 - s + n, n))

        @pl.when(z + 1 + s <= n - 1)
        def _():
            compute(lax.rem(z + 1 + s, n))

    compute_both(0)
    if n < 3:
        cut_out()

    def step(s, carry):
        forward(s)
        compute_both(s)

        @pl.when(s == 1)
        def _():
            cut_out()

        return carry

    lax.fori_loop(1, n - 1, step, 0)

    def finish(owner, carry):
        @pl.when((owner <= z) & (z < n - 1))
        def _():
            to_right(owner).wait_send()

        @pl.when((owner >= z) & (z > 0))
        def _():
            to_left(owner).wait_send()

        to_partner(owner).wait_send()
        return carry

    lax.fori_loop(0, n, finish, 0)

    @pl.when(z > 0)
    def _():
        pl.semaphore_signal(free_r, inc=1, device_id={"tp": lax.rem(z + n - 1, n)}, device_id_type=MESH)

    @pl.when(z < n - 1)
    def _():
        pl.semaphore_signal(free_l, inc=1, device_id={"tp": lax.rem(z + 1, n)}, device_id_type=MESH)

    mine_rows = pl.ds(mult(c * block_rows, 16), block_rows)
    their_rows = pl.ds(mult((1 - c) * block_rows, 16), block_rows)

    def swap(h):
        at = pl.ds(mult(h * HD, 128), HD)
        return pltpu.make_async_remote_copy(
            src_ref=a_ref.at[their_rows, at],
            dst_ref=a_held.at[c, :, at],
            send_sem=pair_send.at[h],
            recv_sem=pair_recv.at[h],
            device_id={"ctx": 1 - c},
            device_id_type=MESH,
        )

    def keep(h):
        at = pl.ds(mult(h * HD, 128), HD)
        return pltpu.make_async_copy(a_ref.at[mine_rows, at], a_held.at[c, :, at], keep_sem.at[h])

    factor = (HD**-0.5) * 1.4426950408889634
    lower = lax.broadcasted_iota(jnp.int32, (block, block), 1) <= lax.broadcasted_iota(
        jnp.int32, (block, block), 0
    )
    turn = (((1,), (1,)), ((), ()))
    power_ref[...] = jnp.zeros_like(power_ref)

    def head(h, carry):
        at = pl.ds(mult(h * HD, 128), HD)
        gain = sub_ref[:, pl.ds(mult(c * cols + h * HD, 128), HD)]
        def finish_rows(here, acc, total):
            att = acc / total
            power_ref[here, :] += att * att
            a_ref[here, at] = (att * gain).astype(BF16)

        def diagonal(here):
            q = qkv_ref[0, here, at]
            diag = lax.dot_general(q, qkv_ref[1, here, at], turn, preferred_element_type=F32)
            return q, jnp.where(lower, diag, low_value)

        def whole_rows(i):
            here = slice(i * block, (i + 1) * block)
            past = slice(0, i * block)
            q, diag = diagonal(here)
            top = jnp.max(diag, axis=-1, keepdims=True)
            if i:
                back = lax.dot_general(q, qkv_ref[1, past, at], turn, preferred_element_type=F32)
                top = jnp.maximum(top, jnp.max(back, axis=-1, keepdims=True))
            e = jnp.exp2((diag - top) * factor)
            total = jnp.sum(e, axis=-1, keepdims=True)
            acc = jnp.dot(e.astype(BF16), qkv_ref[2, here, at], preferred_element_type=F32)
            if i:
                e = jnp.exp2((back - top) * factor)
                total = total + jnp.sum(e, axis=-1, keepdims=True)
                acc = acc + jnp.dot(e.astype(BF16), qkv_ref[2, past, at], preferred_element_type=F32)
            finish_rows(here, acc, total)

        def running_rows(i, carry):
            here = pl.ds(mult(i * block, block), block)
            q, diag = diagonal(here)
            top = jnp.max(diag, axis=-1, keepdims=True)
            e = jnp.exp2((diag - top) * factor)
            total = jnp.sum(e, axis=-1, keepdims=True)
            acc = jnp.dot(e.astype(BF16), qkv_ref[2, here, at], preferred_element_type=F32)

            def back_tile(j, state):
                top, total, acc = state
                past = pl.ds(mult(j * block, block), block)
                back = lax.dot_general(q, qkv_ref[1, past, at], turn, preferred_element_type=F32)
                top_new = jnp.maximum(top, jnp.max(back, axis=-1, keepdims=True))
                e = jnp.exp2((back - top_new) * factor)
                old = jnp.exp2((top - top_new) * factor)
                total = total * old + jnp.sum(e, axis=-1, keepdims=True)
                acc = acc * old + jnp.dot(
                    e.astype(BF16), qkv_ref[2, past, at], preferred_element_type=F32
                )
                return top_new, total, acc

            top, total, acc = lax.fori_loop(0, i, back_tile, (top, total, acc))
            finish_rows(here, acc, total)
            return carry

        q_count = 2 * block_rows // block
        if q_count <= 4:
            for i in range(q_count):
                whole_rows(i)
        else:
            lax.fori_loop(0, q_count, running_rows, 0)
        swap(h).start()
        keep(h).start()
        return carry

    heads = cols // HD
    lax.fori_loop(0, heads, head, 0)

    def sum_tile(b, carry):
        ones = jnp.ones((8, 128), F32)
        blk = power_ref[pl.ds(mult(b * rows, 8), rows), :]
        tiles[b] = lax.dot_general(
            ones, blk, (((1,), (1,)), ((), ())),
            precision=lax.Precision.HIGHEST, preferred_element_type=F32,
        )
        return carry

    lax.fori_loop(0, 2 * n, sum_tile, 0)
    def send_power(j, carry):
        other = lax.rem(c * n + z + j, 2 * n)
        tile_copy(n, c, z, tiles.at[other], psums, ptile_send, ptile_recv, j).start()
        return carry

    lax.fori_loop(1, 2 * n, send_power, 0)

    def arrived(h, carry):
        keep(h).wait()
        swap(h).wait_recv()
        return carry

    lax.fori_loop(0, heads, arrived, 0)

    @pl.when(z > 0)
    def _():
        pl.semaphore_wait(free_l, 1)

    @pl.when(z < n - 1)
    def _():
        pl.semaphore_wait(free_r, 1)

    sum_at = pl.ds(0, rows)
    got_at = pl.ds(rows, rows)

    left = {"tp": lax.rem(z + n - 1, n)}
    right = {"tp": lax.rem(z + 1, n)}

    def move_sum(t, dst, recv, to):
        return pltpu.make_async_remote_copy(
            src_ref=held.at[t, sum_at],
            dst_ref=dst,
            send_sem=send_sem.at[t],
            recv_sem=recv,
            device_id=to,
            device_id_type=MESH,
        )

    def sum_left(t):
        return move_sum(t, held.at[t, got_at], recv_sem.at[t], left)

    def to_right_pass(t):
        return move_sum(t, held.at[t, got_at], recv_sem.at[t], right)

    def to_right_last(t):
        return move_sum(t, extra, extra_sem, right)

    def start_right(t):
        @pl.when(t == z + 1)
        def _():
            to_right_last(t).start()

        @pl.when(t > z + 1)
        def _():
            to_right_pass(t).start()

    tn = min(512, width)
    scale_o = scale_ref[3:4, 0:1].astype(BF16).astype(F32)

    def target(i):
        return lax.select(2 * z >= n, i, n - 1 - i)

    def first(i, carry):
        t = target(i)
        at = pl.ds(mult(t * rows, 16), rows)

        def cols_of(k, inner):
            there = pl.ds(mult(k * tn, 128), tn)
            y = jnp.dot(a_held[0, at, :], wo_held[:cols, there], preferred_element_type=F32)
            y = y + jnp.dot(a_held[1, at, :], wo_held[cols:, there], preferred_element_type=F32)
            held[t, sum_at, there] = (y * scale_o).astype(BF16)
            return inner

        lax.fori_loop(0, width // tn, cols_of, 0)

        @pl.when((z == n - 1) & (t < z))
        def _():
            sum_left(t).start()

        @pl.when((z == 0) & (t > z))
        def _():
            start_right(t)

        return carry

    lax.fori_loop(0, n, first, 0)

    def add_got(t):
        def some(i, inner):
            at = pl.ds(mult(i * 16, 16), 16)
            there = pl.ds(mult(rows + i * 16, 16), 16)
            held[t, at, :] = (
                held[t, at, :].astype(F32) + held[t, there, :].astype(F32)
            ).astype(BF16)
            return inner

        lax.fori_loop(0, rows // 16, some, 0)

    def pass_left(t):
        @pl.when((t < z) & (z < n - 1))
        def _():
            sum_left(t).wait_recv()
            add_got(t)
            sum_left(t).start()

    def pass_right(t):
        @pl.when((t > z) & (z > 0))
        def _():
            to_right_pass(t).wait_recv()
            add_got(t)
            start_right(t)

    def second(i, carry):
        @pl.when(2 * z >= n)
        def _():
            pass_left(i)

        pass_right(n - 1 - i)

        @pl.when(2 * z < n)
        def _():
            pass_left(i)

        return carry

    lax.fori_loop(0, n, second, 0)

    def get_tile(j, acc):
        tile_wait(n, c, z, tiles.at[0], psums, ptile_send, ptile_recv, j).wait_recv()
        return acc + psums[lax.rem(c * n + z + j, 2 * n)]

    power = lax.fori_loop(1, 2 * n, get_tile, tiles[c * n + z]) / width_all
    r = lax.rsqrt(power[0:1, :] + eps_norm)
    r_col = jnp.transpose(jnp.broadcast_to(r, (rows, rows)))
    tiles_of = width // rows
    sums_r = r_col

    @pl.when(z < n - 1)
    def _():
        sum_left(z).wait_recv()

    @pl.when(z > 0)
    def _():
        to_right_last(z).wait_recv()

    @pl.when(z == n - 1)
    def _():
        held[z, got_at, :] = jnp.zeros((rows, width), BF16)

    @pl.when(z == 0)
    def _():
        extra[...] = jnp.zeros((rows, width), BF16)

    def last(k, carry):
        at = pl.ds(mult(k * rows, 128), rows)
        y = held[z, sum_at, at].astype(F32) + held[z, got_at, at].astype(F32) + extra[:, at].astype(F32)
        out_ref[:, at] = (x_ref[:, at].astype(F32) + y * sums_r).astype(BF16)
        return carry

    lax.fori_loop(0, tiles_of, last, 0)

    def finish_sum(t, carry):
        @pl.when(t < z)
        def _():
            sum_left(t).wait_send()

        @pl.when(t > z)
        def _():
            to_right_pass(t).wait_send()

        return carry

    lax.fori_loop(0, n, finish_sum, 0)

    def finish_tile(j, carry):
        tile_wait(n, c, z, part, sums, tile_send, tile_recv, j).wait_send()
        tile_wait(n, c, z, tiles.at[0], psums, ptile_send, ptile_recv, j).wait_send()
        return carry

    lax.fori_loop(1, 2 * n, finish_tile, 0)

    def finish_pair(h, carry):
        swap(h).wait_send()
        return carry

    lax.fori_loop(0, heads, finish_pair, 0)


def body(n, tokens, norm_gain, w_qkv, sub_gain, w_out):
    x = tokens[0]
    rows, width = x.shape
    head_cols = w_qkv.shape[2]
    cols = head_cols // 2
    heads = cols // HD
    all_rows = 2 * n * rows
    count = float(width * n * head_cols)
    pieces = 4
    w = jnp.transpose(w_qkv, (1, 0, 2))
    dma = pltpu.SemaphoreType.DMA
    regular = pltpu.SemaphoreType.REGULAR
    vm = pl.BlockSpec(memory_space=pltpu.VMEM)
    hbm = pl.BlockSpec(memory_space=pl.ANY)
    out = pl.pallas_call(
        functools.partial(layer_kernel, n, count, float(n * head_cols), pieces, 256),
        out_shape=jax.ShapeDtypeStruct((rows, width), BF16),
        in_specs=[vm, vm, hbm, vm, hbm],
        out_specs=vm,
        scratch_shapes=[
            pltpu.VMEM((n, 2 * rows, width), BF16),
            pltpu.VMEM((3, width, cols), BF16),
            pltpu.VMEM(w_out.shape, BF16),
            pltpu.VMEM((3, all_rows, cols), BF16),
            pltpu.VMEM((8, 128), F32),
            pltpu.VMEM((8, 128), F32),
            pltpu.VMEM((2 * n, 8, 128), F32),
            pltpu.VMEM((all_rows, cols), BF16),
            pltpu.VMEM((2, n * rows, cols), BF16),
            pltpu.VMEM((all_rows, HD), F32),
            pltpu.VMEM((rows, width), BF16),
            pltpu.VMEM((2 * n, 8, 128), F32),
            pltpu.VMEM((2 * n, 8, 128), F32),
            dma((4 * pieces,)),
            dma((2 * n,)),
            dma((2 * n,)),
            dma((n,)),
            dma((n,)),
            dma((n,)),
            dma((n,)),
            dma((n,)),
            regular,
            regular,
            dma((heads,)),
            dma((heads,)),
            dma((heads,)),
            dma((2 * n,)),
            dma((2 * n,)),
            dma((n,)),
            dma((n,)),
            dma(()),
        ],
        compiler_params=pltpu.CompilerParams(
            collective_id=0, has_side_effects=True, vmem_limit_bytes=VMEM_LIMIT
        ),
        name="layer",
    )(x, norm_gain.reshape(1, width), w, sub_gain.reshape(1, head_cols), w_out)
    return out[None]


def solution(mesh):
    return jax.shard_map(
        functools.partial(body, mesh.shape["tp"]),
        mesh=mesh,
        in_specs=(P("dp", ("ctx", "tp"), None), P(), P(None, None, "tp"), P("tp"), P("tp", None)),
        out_specs=P("dp", ("ctx", "tp"), None),
        check_vma=False,
    )
```

```python
import functools

import jax
import jax.numpy as jnp
from jax import lax
from jax.experimental import pallas as pl
from jax.experimental.pallas import tpu as pltpu
from jax.sharding import PartitionSpec as P

HD = 128
eps_norm = 1e-05
low_value = -1e30
MESH = pl.DeviceIdType.MESH
F32 = jnp.float32
BF16 = jnp.bfloat16
VMEM_LIMIT = 60 * 1024 * 1024


def mult(x, k):
    return pl.multiple_of(x, k)


def enter(n, c, z):
    barrier = pltpu.get_barrier_semaphore()
    flat = c * n + z

    def greet(j, carry):
        other = lax.rem(flat + j, 2 * n)
        pl.semaphore_signal(
            barrier,
            inc=1,
            device_id={"ctx": other // n, "tp": lax.rem(other, n)},
            device_id_type=MESH,
        )
        return carry

    lax.fori_loop(1, 2 * n, greet, 0)
    pl.semaphore_wait(barrier, 2 * n - 1)


def tile_copy(n, c, z, src, dst, send_sem, recv_sem, j):
    flat = c * n + z
    other = lax.rem(flat + j, 2 * n)
    return pltpu.make_async_remote_copy(
        src_ref=src,
        dst_ref=dst.at[flat],
        send_sem=send_sem.at[other],
        recv_sem=recv_sem.at[flat],
        device_id={"ctx": other // n, "tp": lax.rem(other, n)},
        device_id_type=MESH,
    )


def tile_wait(n, c, z, src, dst, send_sem, recv_sem, j):
    flat = c * n + z
    other = lax.rem(flat + j, 2 * n)
    return pltpu.make_async_remote_copy(
        src_ref=src,
        dst_ref=dst.at[other],
        send_sem=send_sem.at[other],
        recv_sem=recv_sem.at[other],
        device_id={"ctx": other // n, "tp": lax.rem(other, n)},
        device_id_type=MESH,
    )


def layer_kernel(
    n, count, width_all, pieces, block,
    x_ref, gain_ref, w_ref, sub_ref, wo_ref,
    out_ref,
    held, w_held, wo_held, qkv_ref, scale_ref, part, sums,
    a_ref, a_held, power_ref, extra, tiles, psums,
    load_sem, tile_send, tile_recv, send_r, send_l, send_p, recv_z, recv_p,
    free_l, free_r, keep_sem, pair_send, pair_recv, ptile_send, ptile_recv,
    send_sem, recv_sem, extra_sem,
):
    c = lax.axis_index("ctx")
    z = lax.axis_index("tp")
    rows, width = x_ref.shape
    cols = w_held.shape[2]
    deep = width // pieces
    deep_o = wo_held.shape[0] // pieces

    def load_w(m, p):
        return pltpu.make_async_copy(
            w_ref.at[m, pl.ds(p * deep, deep), pl.ds(mult(c * cols, 128), cols)],
            w_held.at[m, pl.ds(p * deep, deep)],
            load_sem.at[m * pieces + p],
        )

    def load_o(p):
        return pltpu.make_async_copy(
            wo_ref.at[pl.ds(p * deep_o, deep_o)],
            wo_held.at[pl.ds(p * deep_o, deep_o)],
            load_sem.at[3 * pieces + p],
        )

    for m in range(3):
        for p in range(pieces):
            load_w(m, p).start()
    for p in range(pieces):
        load_o(p).start()

    mine = mult(c * rows, 16)

    def norm_rows(i, carry):
        x = x_ref[pl.ds(mult(i * 16, 16), 16), :].astype(F32)
        r = lax.rsqrt(jnp.mean(x * x, axis=-1, keepdims=True) + eps_norm)
        held[z, pl.ds(mult(mine + i * 16, 16), 16), :] = (x * r * gain_ref[...]).astype(BF16)
        return carry

    lax.fori_loop(0, rows // 16, norm_rows, 0)
    enter(n, c, z)

    def move(owner, to, send_sem, recv_sem):
        block = held.at[owner, pl.ds(mine, rows)]
        return pltpu.make_async_remote_copy(
            src_ref=block,
            dst_ref=block,
            send_sem=send_sem.at[owner],
            recv_sem=recv_sem.at[owner],
            device_id=to,
            device_id_type=MESH,
        )

    def to_right(owner):
        return move(owner, {"tp": lax.rem(z + 1, n)}, send_r, recv_z)

    def to_left(owner):
        return move(owner, {"tp": lax.rem(z + n - 1, n)}, send_l, recv_z)

    def to_partner(owner):
        return move(owner, {"ctx": 1 - c}, send_p, recv_p)

    def from_partner(owner):
        block = held.at[owner, pl.ds(mult((1 - c) * rows, 16), rows)]
        return pltpu.make_async_remote_copy(
            src_ref=block,
            dst_ref=block,
            send_sem=send_p.at[owner],
            recv_sem=recv_p.at[owner],
            device_id={"ctx": 1 - c},
            device_id_type=MESH,
        )

    def start_own():
        @pl.when(z < n - 1)
        def _():
            to_right(z).start()

        @pl.when(z > 0)
        def _():
            to_left(z).start()

    @pl.when(c == 0)
    def _():
        start_own()

    to_partner(z).start()

    part[...] = jnp.zeros_like(part)
    step_w = 32
    for m in range(3):
        total = jnp.zeros((8, cols), F32)
        for p in range(pieces):
            load_w(m, p).wait()

            def add_w(i, acc, m=m, p=p):
                at = mult(p * deep + i * step_w, step_w)
                v = jnp.abs(w_held[m, pl.ds(at, step_w), :].astype(F32))
                return acc + jnp.sum(v.reshape(step_w // 8, 8, cols), axis=0)

            total = lax.fori_loop(0, deep // step_w, add_w, total)
        one = jnp.sum(jnp.sum(total, axis=0, keepdims=True), axis=1, keepdims=True)
        part[m : m + 1, :] = jnp.broadcast_to(one, (1, 128))
    total = jnp.zeros((8, width), F32)
    for p in range(pieces):
        load_o(p).wait()

        def add_o(i, acc, p=p):
            v = jnp.abs(wo_held[pl.ds(mult(p * deep_o + i * 16, 16), 16), :].astype(F32))
            return acc + jnp.sum(v.reshape(2, 8, width), axis=0)

        total = lax.fori_loop(0, deep_o // 16, add_o, total)
    one = 0.5 * jnp.sum(jnp.sum(total, axis=0, keepdims=True), axis=1, keepdims=True)
    part[3:4, :] = jnp.broadcast_to(one, (1, 128))

    def send_tile(j, carry):
        tile_copy(n, c, z, part, sums, tile_send, tile_recv, j).start()
        return carry

    lax.fori_loop(1, 2 * n, send_tile, 0)

    def forward(s):
        @pl.when(z - 1 - s >= 0)
        def _():
            owner = lax.rem(z - 1 - s + n, n)
            to_right(owner).wait_recv()

            @pl.when(z < n - 1)
            def _():
                to_right(owner).start()

            to_partner(owner).start()

        @pl.when(z + 1 + s <= n - 1)
        def _():
            owner = lax.rem(z + 1 + s, n)
            to_left(owner).wait_recv()

            @pl.when(z > 0)
            def _():
                to_left(owner).start()

            to_partner(owner).start()

    @pl.when(c == 0)
    def _():
        forward(0)

    def get_tile(j, acc):
        tile_wait(n, c, z, part, sums, tile_send, tile_recv, j).wait_recv()
        return acc + sums[lax.rem(c * n + z + j, 2 * n)]

    scale = lax.fori_loop(1, 2 * n, get_tile, part[...]) / count
    scale_ref[...] = scale

    def ternary(w, half):
        one = jnp.ones_like(w)
        zero = jnp.zeros_like(w)
        return jnp.where(w > half, one, jnp.where(w < -half, -one, zero))

    for m in range(3):
        half_w = jnp.broadcast_to((0.5 * scale[m : m + 1, 0:1]).astype(BF16), (step_w, cols))

        def cut_w(i, carry, m=m, half_w=half_w):
            at = pl.ds(mult(i * step_w, step_w), step_w)
            w_held[m, at, :] = ternary(w_held[m, at, :], half_w)
            return carry

        lax.fori_loop(0, width // step_w, cut_w, 0)

    block_rows = n * rows

    def compute(k, owner):
        @pl.when(c != k)
        def _():
            from_partner(owner).wait_recv()

        def one(m, carry):
            s = scale_ref[pl.ds(m, 1), 0:1].astype(BF16).astype(F32)
            y = jnp.dot(
                held[owner, k * rows : (k + 1) * rows, :], w_held[m], preferred_element_type=F32
            )
            at = pl.ds(mult(k * block_rows + owner * rows, 16), rows)
            qkv_ref[m, at, :] = (y * s).astype(BF16)
            return carry

        lax.fori_loop(0, 3, one, 0)

    def compute_at(k, s):
        def side(u, carry):
            owner = lax.select(u == 0, z - s, z + s)

            @pl.when((owner >= 0) & (owner < n) & (u <= s))
            def _():
                compute(k, lax.rem(owner + n, n))

            return carry

        lax.fori_loop(0, 2, side, 0)

    def cut_out():
        half_o = jnp.broadcast_to((0.5 * scale_ref[3:4, 0:1]).astype(BF16), (16, width))

        def cut_o(i, carry):
            at = pl.ds(mult(i * 16, 16), 16)
            wo_held[at, :] = ternary(wo_held[at, :], half_o)
            return carry

        lax.fori_loop(0, wo_held.shape[0] // 16, cut_o, 0)

    def finish_sends():
        def finish(owner, carry):
            @pl.when((owner <= z) & (z < n - 1))
            def _():
                to_right(owner).wait_send()

            @pl.when((owner >= z) & (z > 0))
            def _():
                to_left(owner).wait_send()

            to_partner(owner).wait_send()
            return carry

        lax.fori_loop(0, n, finish, 0)

        @pl.when(z > 0)
        def _():
            pl.semaphore_signal(
                free_r, inc=1, device_id={"tp": lax.rem(z + n - 1, n)}, device_id_type=MESH
            )

        @pl.when(z < n - 1)
        def _():
            pl.semaphore_signal(
                free_l, inc=1, device_id={"tp": lax.rem(z + 1, n)}, device_id_type=MESH
            )

    mine_rows = pl.ds(mult(c * block_rows, 16), block_rows)
    their_rows = pl.ds(mult((1 - c) * block_rows, 16), block_rows)

    def swap(h):
        at = pl.ds(mult(h * HD, 128), HD)
        return pltpu.make_async_remote_copy(
            src_ref=a_ref.at[their_rows, at],
            dst_ref=a_held.at[c, :, at],
            send_sem=pair_send.at[h],
            recv_sem=pair_recv.at[h],
            device_id={"ctx": 1 - c},
            device_id_type=MESH,
        )

    def keep(h):
        at = pl.ds(mult(h * HD, 128), HD)
        return pltpu.make_async_copy(a_ref.at[mine_rows, at], a_held.at[c, :, at], keep_sem.at[h])

    factor = (HD**-0.5) * 1.4426950408889634
    lower = lax.broadcasted_iota(jnp.int32, (block, block), 1) <= lax.broadcasted_iota(
        jnp.int32, (block, block), 0
    )
    turn = (((1,), (1,)), ((), ()))
    power_ref[...] = jnp.zeros_like(power_ref)
    heads = cols // HD
    half = block_rows // block

    def head(k, h):
        at = pl.ds(mult(h * HD, 128), HD)
        gain = sub_ref[:, pl.ds(mult(c * cols + h * HD, 128), HD)]
        def finish_rows(here, acc, total):
            att = acc / total
            power_ref[here, :] += att * att
            a_ref[here, at] = (att * gain).astype(BF16)

        def diagonal(here):
            q = qkv_ref[0, here, at]
            diag = lax.dot_general(q, qkv_ref[1, here, at], turn, preferred_element_type=F32)
            return q, jnp.where(lower, diag, low_value)

        def whole_rows(i):
            here = slice(i * block, (i + 1) * block)
            past = slice(0, i * block)
            q, diag = diagonal(here)
            top = jnp.max(diag, axis=-1, keepdims=True)
            if i:
                back = lax.dot_general(q, qkv_ref[1, past, at], turn, preferred_element_type=F32)
                top = jnp.maximum(top, jnp.max(back, axis=-1, keepdims=True))
            e = jnp.exp2((diag - top) * factor)
            total = jnp.sum(e, axis=-1, keepdims=True)
            acc = jnp.dot(e.astype(BF16), qkv_ref[2, here, at], preferred_element_type=F32)
            if i:
                e = jnp.exp2((back - top) * factor)
                total = total + jnp.sum(e, axis=-1, keepdims=True)
                acc = acc + jnp.dot(e.astype(BF16), qkv_ref[2, past, at], preferred_element_type=F32)
            finish_rows(here, acc, total)

        def running_rows(i, carry):
            here = pl.ds(mult(i * block, block), block)
            q, diag = diagonal(here)
            top = jnp.max(diag, axis=-1, keepdims=True)
            e = jnp.exp2((diag - top) * factor)
            total = jnp.sum(e, axis=-1, keepdims=True)
            acc = jnp.dot(e.astype(BF16), qkv_ref[2, here, at], preferred_element_type=F32)

            def back_tile(j, state):
                top, total, acc = state
                past = pl.ds(mult(j * block, block), block)
                back = lax.dot_general(q, qkv_ref[1, past, at], turn, preferred_element_type=F32)
                top_new = jnp.maximum(top, jnp.max(back, axis=-1, keepdims=True))
                e = jnp.exp2((back - top_new) * factor)
                old = jnp.exp2((top - top_new) * factor)
                total = total * old + jnp.sum(e, axis=-1, keepdims=True)
                acc = acc * old + jnp.dot(
                    e.astype(BF16), qkv_ref[2, past, at], preferred_element_type=F32
                )
                return top_new, total, acc

            top, total, acc = lax.fori_loop(0, i, back_tile, (top, total, acc))
            finish_rows(here, acc, total)
            return carry

        if 2 * half <= 4:
            for i in range(k * half, (k + 1) * half):
                whole_rows(i)
        else:
            lax.fori_loop(k * half, (k + 1) * half, running_rows, 0)

        @pl.when(c != k)
        def _():
            swap(h).start()

        @pl.when(c == k)
        def _():
            keep(h).start()

    flat = c * n + z

    def attend(k):
        def one_head(h, carry):
            head(k, h)
            return carry

        lax.fori_loop(0, heads, one_head, 0)

        def power_tile(j, carry):
            b = k * n + j
            ones = jnp.ones((8, 128), F32)
            blk = power_ref[pl.ds(mult(b * rows, 8), rows), :]
            tiles[b] = lax.dot_general(
                ones, blk, (((1,), (1,)), ((), ())),
                precision=lax.Precision.HIGHEST, preferred_element_type=F32,
            )

            @pl.when(b != flat)
            def _():
                step = lax.rem(b - flat + 2 * n, 2 * n)
                tile_copy(n, c, z, tiles.at[b], psums, ptile_send, ptile_recv, step).start()

            return carry

        lax.fori_loop(0, n, power_tile, 0)

    region = pl.ds(mine, rows)
    left = {"tp": lax.rem(z + n - 1, n)}
    right = {"tp": lax.rem(z + 1, n)}

    def move_sum(t, dst, recv, to):
        return pltpu.make_async_remote_copy(
            src_ref=held.at[t, region],
            dst_ref=dst,
            send_sem=send_sem.at[t],
            recv_sem=recv,
            device_id=to,
            device_id_type=MESH,
        )

    def sum_left(t):
        return move_sum(t, held.at[t, region], recv_sem.at[t], left)

    def sum_right(t):
        return move_sum(t, held.at[t, region], recv_sem.at[t], right)

    def sum_right_last(t):
        return move_sum(t, extra, extra_sem, right)

    def start_sum(t):
        @pl.when(t < z)
        def _():
            sum_left(t).start()

        @pl.when(t == z + 1)
        def _():
            sum_right_last(t).start()

        @pl.when(t > z + 1)
        def _():
            sum_right(t).start()

    tn = min(512, width)

    def product(t, there):
        at = pl.ds(mult(t * rows, 16), rows)
        y = jnp.dot(a_held[0, at, :], wo_held[:cols, there], preferred_element_type=F32)
        y = y + jnp.dot(a_held[1, at, :], wo_held[cols:, there], preferred_element_type=F32)
        return (y * scale_ref[3:4, 0:1].astype(BF16).astype(F32)).astype(BF16)

    def partial(t, add):
        def cols_of(k, carry):
            there = pl.ds(mult(k * tn, 128), tn)
            y = product(t, there)
            if add:
                y = (y.astype(F32) + held[t, region, there].astype(F32)).astype(BF16)
            held[t, region, there] = y
            return carry

        lax.fori_loop(0, width // tn, cols_of, 0)

    def sums_begin():
        def arrived(h, carry):
            keep(h).wait()
            swap(h).wait_recv()
            return carry

        lax.fori_loop(0, heads, arrived, 0)

        @pl.when(z > 0)
        def _():
            pl.semaphore_wait(free_l, 1)

        @pl.when(z < n - 1)
        def _():
            pl.semaphore_wait(free_r, 1)

        def first(i, carry):
            t = lax.select(2 * z >= n, i, n - 1 - i)

            @pl.when(((z == n - 1) & (t < z)) | ((z == 0) & (t > z)))
            def _():
                partial(t, False)
                start_sum(t)

            return carry

        lax.fori_loop(0, n, first, 0)

    def sums_step(i):
        def way(u, carry):
            t = lax.select((2 * z >= n) == (u == 0), i, n - 1 - i)
            is_left = (2 * z >= n) == (u == 0)

            @pl.when((is_left & (t < z) & (z < n - 1)) | ((~is_left) & (t > z) & (z > 0)))
            def _():
                sum_left(t).wait_recv()
                partial(t, True)
                start_sum(t)

            return carry

        lax.fori_loop(0, 2, way, 0)

    compute_at(0, 0)
    compute_at(0, 1)
    if n < 3:
        cut_out()

    def step(s, carry):
        @pl.when(c == 0)
        def _():
            forward(s - 1)

        compute_at(0, s)

        @pl.when(s == 2)
        def _():
            cut_out()

        return carry

    lax.fori_loop(2, n, step, 0)

    @pl.when(c == 1)
    def _():
        start_own()

    @pl.when(c == 0)
    def _():
        finish_sends()

    attend(0)

    @pl.when(c == 0)
    def _():
        sums_begin()

    def step_one(s, carry):
        @pl.when((c == 1) & (s >= 1))
        def _():
            forward(s - 1)

        compute_at(1, s)

        @pl.when(c == 0)
        def _():
            sums_step(s)

        return carry

    lax.fori_loop(0, n, step_one, 0)

    @pl.when(c == 1)
    def _():
        finish_sends()

    attend(1)

    @pl.when(c == 1)
    def _():
        sums_begin()

        def step_two(s, carry):
            sums_step(s)
            return carry

        lax.fori_loop(0, n, step_two, 0)

    def get_power(j, acc):
        tile_wait(n, c, z, tiles.at[0], psums, ptile_send, ptile_recv, j).wait_recv()
        return acc + psums[lax.rem(flat + j, 2 * n)]

    power = lax.fori_loop(1, 2 * n, get_power, tiles[flat]) / width_all
    r = lax.rsqrt(power[0:1, :] + eps_norm)
    r_col = jnp.transpose(jnp.broadcast_to(r, (rows, rows)))

    @pl.when(z < n - 1)
    def _():
        sum_left(z).wait_recv()

    @pl.when(z > 0)
    def _():
        sum_right_last(z).wait_recv()

    @pl.when(z == n - 1)
    def _():
        held[z, region, :] = jnp.zeros((rows, width), BF16)

    @pl.when(z == 0)
    def _():
        extra[...] = jnp.zeros((rows, width), BF16)

    r_wide = jnp.concatenate([r_col] * (tn // rows), axis=1)

    def last(k, carry):
        at = pl.ds(mult(k * tn, 128), tn)
        y = product(z, at).astype(F32) + held[z, region, at].astype(F32) + extra[:, at].astype(F32)
        out_ref[:, at] = (x_ref[:, at].astype(F32) + y * r_wide).astype(BF16)
        return carry

    lax.fori_loop(0, width // tn, last, 0)

    def finish_sum(t, carry):
        @pl.when(t != z)
        def _():
            sum_left(t).wait_send()

        return carry

    lax.fori_loop(0, n, finish_sum, 0)

    def finish_tile(j, carry):
        tile_wait(n, c, z, part, sums, tile_send, tile_recv, j).wait_send()
        tile_wait(n, c, z, tiles.at[0], psums, ptile_send, ptile_recv, j).wait_send()
        return carry

    lax.fori_loop(1, 2 * n, finish_tile, 0)

    def finish_pair(h, carry):
        swap(h).wait_send()
        return carry

    lax.fori_loop(0, heads, finish_pair, 0)


def body(n, tokens, norm_gain, w_qkv, sub_gain, w_out):
    x = tokens[0]
    rows, width = x.shape
    head_cols = w_qkv.shape[2]
    cols = head_cols // 2
    heads = cols // HD
    all_rows = 2 * n * rows
    count = float(width * n * head_cols)
    pieces = 4
    w = jnp.transpose(w_qkv, (1, 0, 2))
    dma = pltpu.SemaphoreType.DMA
    regular = pltpu.SemaphoreType.REGULAR
    vm = pl.BlockSpec(memory_space=pltpu.VMEM)
    hbm = pl.BlockSpec(memory_space=pl.ANY)
    out = pl.pallas_call(
        functools.partial(layer_kernel, n, count, float(n * head_cols), pieces, 256),
        out_shape=jax.ShapeDtypeStruct((rows, width), BF16),
        in_specs=[vm, vm, hbm, vm, hbm],
        out_specs=vm,
        scratch_shapes=[
            pltpu.VMEM((n, 2 * rows, width), BF16),
            pltpu.VMEM((3, width, cols), BF16),
            pltpu.VMEM(w_out.shape, BF16),
            pltpu.VMEM((3, all_rows, cols), BF16),
            pltpu.VMEM((8, 128), F32),
            pltpu.VMEM((8, 128), F32),
            pltpu.VMEM((2 * n, 8, 128), F32),
            pltpu.VMEM((all_rows, cols), BF16),
            pltpu.VMEM((2, n * rows, cols), BF16),
            pltpu.VMEM((all_rows, HD), F32),
            pltpu.VMEM((rows, width), BF16),
            pltpu.VMEM((2 * n, 8, 128), F32),
            pltpu.VMEM((2 * n, 8, 128), F32),
            dma((4 * pieces,)),
            dma((2 * n,)),
            dma((2 * n,)),
            dma((n,)),
            dma((n,)),
            dma((n,)),
            dma((n,)),
            dma((n,)),
            regular,
            regular,
            dma((heads,)),
            dma((heads,)),
            dma((heads,)),
            dma((2 * n,)),
            dma((2 * n,)),
            dma((n,)),
            dma((n,)),
            dma(()),
        ],
        compiler_params=pltpu.CompilerParams(
            collective_id=0, has_side_effects=True, vmem_limit_bytes=VMEM_LIMIT
        ),
        name="layer",
    )(x, norm_gain.reshape(1, width), w, sub_gain.reshape(1, head_cols), w_out)
    return out[None]


def solution(mesh):
    return jax.shard_map(
        functools.partial(body, mesh.shape["tp"]),
        mesh=mesh,
        in_specs=(P("dp", ("ctx", "tp"), None), P(), P(None, None, "tp"), P("tp"), P("tp", None)),
        out_specs=P("dp", ("ctx", "tp"), None),
        check_vma=False,
    )
```

```python
import functools

import jax
import jax.numpy as jnp
from jax import lax
from jax.experimental import pallas as pl
from jax.experimental.pallas import tpu as pltpu
from jax.sharding import PartitionSpec as P

HD = 128
eps_norm = 1e-05
low_value = -1e30
MESH = pl.DeviceIdType.MESH
F32 = jnp.float32
BF16 = jnp.bfloat16
VMEM_LIMIT = 60 * 1024 * 1024


def mult(x, k):
    return pl.multiple_of(x, k)


def enter(n, c, z):
    barrier = pltpu.get_barrier_semaphore()
    flat = c * n + z

    def greet(j, carry):
        other = lax.rem(flat + j, 2 * n)
        pl.semaphore_signal(
            barrier,
            inc=1,
            device_id={"ctx": other // n, "tp": lax.rem(other, n)},
            device_id_type=MESH,
        )
        return carry

    lax.fori_loop(1, 2 * n, greet, 0)
    pl.semaphore_wait(barrier, 2 * n - 1)


def tile_copy(n, c, z, src, dst, send_sem, recv_sem, j):
    flat = c * n + z
    other = lax.rem(flat + j, 2 * n)
    return pltpu.make_async_remote_copy(
        src_ref=src,
        dst_ref=dst.at[flat],
        send_sem=send_sem.at[other],
        recv_sem=recv_sem.at[flat],
        device_id={"ctx": other // n, "tp": lax.rem(other, n)},
        device_id_type=MESH,
    )


def tile_wait(n, c, z, src, dst, send_sem, recv_sem, j):
    flat = c * n + z
    other = lax.rem(flat + j, 2 * n)
    return pltpu.make_async_remote_copy(
        src_ref=src,
        dst_ref=dst.at[other],
        send_sem=send_sem.at[other],
        recv_sem=recv_sem.at[other],
        device_id={"ctx": other // n, "tp": lax.rem(other, n)},
        device_id_type=MESH,
    )


def layer_kernel(
    n, count, width_all, pieces, block,
    x_ref, gain_ref, w_ref, sub_ref, wo_ref,
    out_ref,
    held, w_held, wo_held, qkv_ref, scale_ref, part, sums,
    a_ref, a_held, power_ref, extra, tiles, psums,
    load_sem, tile_send, tile_recv, send_r, send_l, send_p, recv_z, recv_p,
    free_l, free_r, keep_sem, pair_send, pair_recv, ptile_send, ptile_recv,
    send_sem, recv_sem, extra_sem,
):
    c = lax.axis_index("ctx")
    z = lax.axis_index("tp")
    rows, width = x_ref.shape
    cols = w_held.shape[2]
    deep = width // pieces
    deep_o = wo_held.shape[0] // pieces

    def load_w(m, p):
        return pltpu.make_async_copy(
            w_ref.at[m, pl.ds(p * deep, deep), pl.ds(mult(c * cols, 128), cols)],
            w_held.at[m, pl.ds(p * deep, deep)],
            load_sem.at[m * pieces + p],
        )

    def load_o(p):
        return pltpu.make_async_copy(
            wo_ref.at[pl.ds(p * deep_o, deep_o)],
            wo_held.at[pl.ds(p * deep_o, deep_o)],
            load_sem.at[3 * pieces + p],
        )

    for m in range(3):
        for p in range(pieces):
            load_w(m, p).start()
    for p in range(pieces):
        load_o(p).start()

    mine = mult(c * rows, 16)

    def norm_rows(i, carry):
        x = x_ref[pl.ds(mult(i * 16, 16), 16), :].astype(F32)
        r = lax.rsqrt(jnp.mean(x * x, axis=-1, keepdims=True) + eps_norm)
        held[z, pl.ds(mult(mine + i * 16, 16), 16), :] = (x * r * gain_ref[...]).astype(BF16)
        return carry

    lax.fori_loop(0, rows // 16, norm_rows, 0)
    enter(n, c, z)

    def move(owner, to, send_sem, recv_sem):
        block = held.at[owner, pl.ds(mine, rows)]
        return pltpu.make_async_remote_copy(
            src_ref=block,
            dst_ref=block,
            send_sem=send_sem.at[owner],
            recv_sem=recv_sem.at[owner],
            device_id=to,
            device_id_type=MESH,
        )

    def to_right(owner):
        return move(owner, {"tp": lax.rem(z + 1, n)}, send_r, recv_z)

    def to_left(owner):
        return move(owner, {"tp": lax.rem(z + n - 1, n)}, send_l, recv_z)

    def to_partner(owner):
        return move(owner, {"ctx": 1 - c}, send_p, recv_p)

    def from_partner(owner):
        block = held.at[owner, pl.ds(mult((1 - c) * rows, 16), rows)]
        return pltpu.make_async_remote_copy(
            src_ref=block,
            dst_ref=block,
            send_sem=send_p.at[owner],
            recv_sem=recv_p.at[owner],
            device_id={"ctx": 1 - c},
            device_id_type=MESH,
        )

    def start_own():
        @pl.when(z < n - 1)
        def _():
            to_right(z).start()

        @pl.when(z > 0)
        def _():
            to_left(z).start()

    @pl.when(c == 0)
    def _():
        start_own()

    to_partner(z).start()

    part[...] = jnp.zeros_like(part)
    step_w = 32
    for m in range(3):
        total = jnp.zeros((8, cols), F32)
        for p in range(pieces):
            load_w(m, p).wait()

            def add_w(i, acc, m=m, p=p):
                at = mult(p * deep + i * step_w, step_w)
                v = jnp.abs(w_held[m, pl.ds(at, step_w), :].astype(F32))
                return acc + jnp.sum(v.reshape(step_w // 8, 8, cols), axis=0)

            total = lax.fori_loop(0, deep // step_w, add_w, total)
        one = jnp.sum(jnp.sum(total, axis=0, keepdims=True), axis=1, keepdims=True)
        part[m : m + 1, :] = jnp.broadcast_to(one, (1, 128))
    total = jnp.zeros((8, width), F32)
    for p in range(pieces):
        load_o(p).wait()

        def add_o(i, acc, p=p):
            v = jnp.abs(wo_held[pl.ds(mult(p * deep_o + i * 16, 16), 16), :].astype(F32))
            return acc + jnp.sum(v.reshape(2, 8, width), axis=0)

        total = lax.fori_loop(0, deep_o // 16, add_o, total)
    one = 0.5 * jnp.sum(jnp.sum(total, axis=0, keepdims=True), axis=1, keepdims=True)
    part[3:4, :] = jnp.broadcast_to(one, (1, 128))

    def send_tile(j, carry):
        tile_copy(n, c, z, part, sums, tile_send, tile_recv, j).start()
        return carry

    lax.fori_loop(1, 2 * n, send_tile, 0)

    def forward(s):
        @pl.when(z - 1 - s >= 0)
        def _():
            owner = lax.rem(z - 1 - s + n, n)
            to_right(owner).wait_recv()

            @pl.when(z < n - 1)
            def _():
                to_right(owner).start()

            to_partner(owner).start()

        @pl.when(z + 1 + s <= n - 1)
        def _():
            owner = lax.rem(z + 1 + s, n)
            to_left(owner).wait_recv()

            @pl.when(z > 0)
            def _():
                to_left(owner).start()

            to_partner(owner).start()

    @pl.when(c == 0)
    def _():
        forward(0)

    def get_tile(j, acc):
        tile_wait(n, c, z, part, sums, tile_send, tile_recv, j).wait_recv()
        return acc + sums[lax.rem(c * n + z + j, 2 * n)]

    scale = lax.fori_loop(1, 2 * n, get_tile, part[...]) / count
    scale_ref[...] = scale

    def ternary(w, half):
        one = jnp.ones_like(w)
        zero = jnp.zeros_like(w)
        return jnp.where(w > half, one, jnp.where(w < -half, -one, zero))

    for m in range(3):
        half_w = jnp.broadcast_to((0.5 * scale[m : m + 1, 0:1]).astype(BF16), (step_w, cols))

        def cut_w(i, carry, m=m, half_w=half_w):
            at = pl.ds(mult(i * step_w, step_w), step_w)
            w_held[m, at, :] = ternary(w_held[m, at, :], half_w)
            return carry

        lax.fori_loop(0, width // step_w, cut_w, 0)

    block_rows = n * rows

    def compute(k, owner):
        @pl.when(c != k)
        def _():
            from_partner(owner).wait_recv()

        def one(m, carry):
            s = scale_ref[pl.ds(m, 1), 0:1].astype(BF16).astype(F32)
            y = jnp.dot(
                held[owner, k * rows : (k + 1) * rows, :], w_held[m], preferred_element_type=F32
            )
            at = pl.ds(mult(k * block_rows + owner * rows, 16), rows)
            qkv_ref[m, at, :] = (y * s).astype(BF16)
            return carry

        lax.fori_loop(0, 3, one, 0)

    def compute_at(k, s):
        def side(u, carry):
            owner = lax.select(u == 0, z - s, z + s)

            @pl.when((owner >= 0) & (owner < n) & (u <= s))
            def _():
                compute(k, lax.rem(owner + n, n))

            return carry

        lax.fori_loop(0, 2, side, 0)

    def cut_out():
        half_o = jnp.broadcast_to((0.5 * scale_ref[3:4, 0:1]).astype(BF16), (16, width))

        def cut_o(i, carry):
            at = pl.ds(mult(i * 16, 16), 16)
            wo_held[at, :] = ternary(wo_held[at, :], half_o)
            return carry

        lax.fori_loop(0, wo_held.shape[0] // 16, cut_o, 0)

    def finish_sends():
        def finish(owner, carry):
            @pl.when((owner <= z) & (z < n - 1))
            def _():
                to_right(owner).wait_send()

            @pl.when((owner >= z) & (z > 0))
            def _():
                to_left(owner).wait_send()

            to_partner(owner).wait_send()
            return carry

        lax.fori_loop(0, n, finish, 0)

        @pl.when(z > 0)
        def _():
            pl.semaphore_signal(
                free_r, inc=1, device_id={"tp": lax.rem(z + n - 1, n)}, device_id_type=MESH
            )

        @pl.when(z < n - 1)
        def _():
            pl.semaphore_signal(
                free_l, inc=1, device_id={"tp": lax.rem(z + 1, n)}, device_id_type=MESH
            )

    mine_rows = pl.ds(mult(c * block_rows, 16), block_rows)
    their_rows = pl.ds(mult((1 - c) * block_rows, 16), block_rows)

    def swap(h):
        at = pl.ds(mult(h * HD, 128), HD)
        return pltpu.make_async_remote_copy(
            src_ref=a_ref.at[their_rows, at],
            dst_ref=a_held.at[c, :, at],
            send_sem=pair_send.at[h],
            recv_sem=pair_recv.at[h],
            device_id={"ctx": 1 - c},
            device_id_type=MESH,
        )

    def keep(h):
        at = pl.ds(mult(h * HD, 128), HD)
        return pltpu.make_async_copy(a_ref.at[mine_rows, at], a_held.at[c, :, at], keep_sem.at[h])

    factor = (HD**-0.5) * 1.4426950408889634
    lower = lax.broadcasted_iota(jnp.int32, (block, block), 1) <= lax.broadcasted_iota(
        jnp.int32, (block, block), 0
    )
    turn = (((1,), (1,)), ((), ()))
    power_ref[...] = jnp.zeros_like(power_ref)
    heads = cols // HD
    half = block_rows // block

    def head(k, h):
        at = pl.ds(mult(h * HD, 128), HD)
        gain = sub_ref[:, pl.ds(mult(c * cols + h * HD, 128), HD)]
        def finish_rows(here, acc, total):
            att = acc / total
            power_ref[here, :] += att * att
            a_ref[here, at] = (att * gain).astype(BF16)

        def diagonal(here):
            q = qkv_ref[0, here, at]
            diag = lax.dot_general(q, qkv_ref[1, here, at], turn, preferred_element_type=F32)
            return q, jnp.where(lower, diag, low_value)

        def whole_rows(i):
            here = slice(i * block, (i + 1) * block)
            past = slice(0, i * block)
            q, diag = diagonal(here)
            top = jnp.max(diag, axis=-1, keepdims=True)
            if i:
                back = lax.dot_general(q, qkv_ref[1, past, at], turn, preferred_element_type=F32)
                top = jnp.maximum(top, jnp.max(back, axis=-1, keepdims=True))
            e = jnp.exp2((diag - top) * factor)
            total = jnp.sum(e, axis=-1, keepdims=True)
            acc = jnp.dot(e.astype(BF16), qkv_ref[2, here, at], preferred_element_type=F32)
            if i:
                e = jnp.exp2((back - top) * factor)
                total = total + jnp.sum(e, axis=-1, keepdims=True)
                acc = acc + jnp.dot(e.astype(BF16), qkv_ref[2, past, at], preferred_element_type=F32)
            finish_rows(here, acc, total)

        def running_rows(i, carry):
            here = pl.ds(mult(i * block, block), block)
            q, diag = diagonal(here)
            top = jnp.max(diag, axis=-1, keepdims=True)
            e = jnp.exp2((diag - top) * factor)
            total = jnp.sum(e, axis=-1, keepdims=True)
            acc = jnp.dot(e.astype(BF16), qkv_ref[2, here, at], preferred_element_type=F32)

            def back_tile(j, state):
                top, total, acc = state
                past = pl.ds(mult(j * block, block), block)
                back = lax.dot_general(q, qkv_ref[1, past, at], turn, preferred_element_type=F32)
                top_new = jnp.maximum(top, jnp.max(back, axis=-1, keepdims=True))
                e = jnp.exp2((back - top_new) * factor)
                old = jnp.exp2((top - top_new) * factor)
                total = total * old + jnp.sum(e, axis=-1, keepdims=True)
                acc = acc * old + jnp.dot(
                    e.astype(BF16), qkv_ref[2, past, at], preferred_element_type=F32
                )
                return top_new, total, acc

            top, total, acc = lax.fori_loop(0, i, back_tile, (top, total, acc))
            finish_rows(here, acc, total)
            return carry

        if 2 * half <= 4:
            for i in range(k * half, (k + 1) * half):
                whole_rows(i)
        else:
            lax.fori_loop(k * half, (k + 1) * half, running_rows, 0)

        @pl.when(c != k)
        def _():
            swap(h).start()

        @pl.when(c == k)
        def _():
            keep(h).start()

    flat = c * n + z

    def attend(k):
        def one_head(h, carry):
            head(k, h)
            return carry

        lax.fori_loop(0, heads, one_head, 0)

        def power_tile(j, carry):
            b = k * n + j
            ones = jnp.ones((8, 128), F32)
            blk = power_ref[pl.ds(mult(b * rows, 8), rows), :]
            tiles[b] = lax.dot_general(
                ones, blk, (((1,), (1,)), ((), ())),
                precision=lax.Precision.HIGHEST, preferred_element_type=F32,
            )

            @pl.when(b != flat)
            def _():
                step = lax.rem(b - flat + 2 * n, 2 * n)
                tile_copy(n, c, z, tiles.at[b], psums, ptile_send, ptile_recv, step).start()

            return carry

        lax.fori_loop(0, n, power_tile, 0)

    region = pl.ds(mine, rows)
    left = {"tp": lax.rem(z + n - 1, n)}
    right = {"tp": lax.rem(z + 1, n)}

    def move_sum(t, dst, recv, to):
        return pltpu.make_async_remote_copy(
            src_ref=held.at[t, region],
            dst_ref=dst,
            send_sem=send_sem.at[t],
            recv_sem=recv,
            device_id=to,
            device_id_type=MESH,
        )

    def sum_left(t):
        return move_sum(t, held.at[t, region], recv_sem.at[t], left)

    def sum_right(t):
        return move_sum(t, held.at[t, region], recv_sem.at[t], right)

    def sum_right_last(t):
        return move_sum(t, extra, extra_sem, right)

    def start_sum(t):
        @pl.when(t < z)
        def _():
            sum_left(t).start()

        @pl.when(t == z + 1)
        def _():
            sum_right_last(t).start()

        @pl.when(t > z + 1)
        def _():
            sum_right(t).start()

    tn = min(512, width)

    def product(t, there):
        at = pl.ds(mult(t * rows, 16), rows)
        y = jnp.dot(a_held[0, at, :], wo_held[:cols, there], preferred_element_type=F32)
        y = y + jnp.dot(a_held[1, at, :], wo_held[cols:, there], preferred_element_type=F32)
        return (y * scale_ref[3:4, 0:1].astype(BF16).astype(F32)).astype(BF16)

    def partial(t, add):
        def cols_of(k, carry):
            there = pl.ds(mult(k * tn, 128), tn)
            y = product(t, there)
            if add:
                y = (y.astype(F32) + held[t, region, there].astype(F32)).astype(BF16)
            held[t, region, there] = y
            return carry

        lax.fori_loop(0, width // tn, cols_of, 0)

    def sums_begin():
        def arrived(h, carry):
            keep(h).wait()
            swap(h).wait_recv()
            return carry

        lax.fori_loop(0, heads, arrived, 0)

        @pl.when(z > 0)
        def _():
            pl.semaphore_wait(free_l, 1)

        @pl.when(z < n - 1)
        def _():
            pl.semaphore_wait(free_r, 1)

        def first(i, carry):
            t = lax.select(2 * z >= n, i, n - 1 - i)

            @pl.when(((z == n - 1) & (t < z)) | ((z == 0) & (t > z)))
            def _():
                partial(t, False)
                start_sum(t)

            return carry

        lax.fori_loop(0, n, first, 0)

    def sums_step(i):
        def way(u, carry):
            t = lax.select((2 * z >= n) == (u == 0), i, n - 1 - i)
            is_left = (2 * z >= n) == (u == 0)

            @pl.when((is_left & (t < z) & (z < n - 1)) | ((~is_left) & (t > z) & (z > 0)))
            def _():
                sum_left(t).wait_recv()
                partial(t, True)
                start_sum(t)

            return carry

        lax.fori_loop(0, 2, way, 0)

    compute_at(0, 0)
    compute_at(0, 1)

    @pl.when(c == 1)
    def _():
        start_own()

    if n < 3:
        cut_out()

    def step(s, carry):
        @pl.when(c == 0)
        def _():
            forward(s - 1)

        compute_at(0, s)

        @pl.when(s == 2)
        def _():
            cut_out()

        return carry

    lax.fori_loop(2, n, step, 0)

    @pl.when(c == 0)
    def _():
        finish_sends()

    attend(0)

    @pl.when(c == 0)
    def _():
        sums_begin()

    def step_one(s, carry):
        @pl.when((c == 1) & (s >= 1))
        def _():
            forward(s - 1)

        compute_at(1, s)

        @pl.when(c == 0)
        def _():
            sums_step(s)

        return carry

    lax.fori_loop(0, n, step_one, 0)

    @pl.when(c == 1)
    def _():
        finish_sends()

    attend(1)

    @pl.when(c == 1)
    def _():
        sums_begin()

        def step_two(s, carry):
            sums_step(s)
            return carry

        lax.fori_loop(0, n, step_two, 0)

    def get_power(j, acc):
        tile_wait(n, c, z, tiles.at[0], psums, ptile_send, ptile_recv, j).wait_recv()
        return acc + psums[lax.rem(flat + j, 2 * n)]

    power = lax.fori_loop(1, 2 * n, get_power, tiles[flat]) / width_all
    r = lax.rsqrt(power[0:1, :] + eps_norm)
    r_col = jnp.transpose(jnp.broadcast_to(r, (rows, rows)))

    @pl.when(z < n - 1)
    def _():
        sum_left(z).wait_recv()

    @pl.when(z > 0)
    def _():
        sum_right_last(z).wait_recv()

    @pl.when(z == n - 1)
    def _():
        held[z, region, :] = jnp.zeros((rows, width), BF16)

    @pl.when(z == 0)
    def _():
        extra[...] = jnp.zeros((rows, width), BF16)

    r_wide = jnp.concatenate([r_col] * (tn // rows), axis=1)

    def last(k, carry):
        at = pl.ds(mult(k * tn, 128), tn)
        y = product(z, at).astype(F32) + held[z, region, at].astype(F32) + extra[:, at].astype(F32)
        out_ref[:, at] = (x_ref[:, at].astype(F32) + y * r_wide).astype(BF16)
        return carry

    lax.fori_loop(0, width // tn, last, 0)

    def finish_sum(t, carry):
        @pl.when(t != z)
        def _():
            sum_left(t).wait_send()

        return carry

    lax.fori_loop(0, n, finish_sum, 0)

    def finish_tile(j, carry):
        tile_wait(n, c, z, part, sums, tile_send, tile_recv, j).wait_send()
        tile_wait(n, c, z, tiles.at[0], psums, ptile_send, ptile_recv, j).wait_send()
        return carry

    lax.fori_loop(1, 2 * n, finish_tile, 0)

    def finish_pair(h, carry):
        swap(h).wait_send()
        return carry

    lax.fori_loop(0, heads, finish_pair, 0)


def body(n, tokens, norm_gain, w_qkv, sub_gain, w_out):
    x = tokens[0]
    rows, width = x.shape
    head_cols = w_qkv.shape[2]
    cols = head_cols // 2
    heads = cols // HD
    all_rows = 2 * n * rows
    count = float(width * n * head_cols)
    pieces = 4
    w = jnp.transpose(w_qkv, (1, 0, 2))
    dma = pltpu.SemaphoreType.DMA
    regular = pltpu.SemaphoreType.REGULAR
    vm = pl.BlockSpec(memory_space=pltpu.VMEM)
    hbm = pl.BlockSpec(memory_space=pl.ANY)
    out = pl.pallas_call(
        functools.partial(layer_kernel, n, count, float(n * head_cols), pieces, 256),
        out_shape=jax.ShapeDtypeStruct((rows, width), BF16),
        in_specs=[vm, vm, hbm, vm, hbm],
        out_specs=vm,
        scratch_shapes=[
            pltpu.VMEM((n, 2 * rows, width), BF16),
            pltpu.VMEM((3, width, cols), BF16),
            pltpu.VMEM(w_out.shape, BF16),
            pltpu.VMEM((3, all_rows, cols), BF16),
            pltpu.VMEM((8, 128), F32),
            pltpu.VMEM((8, 128), F32),
            pltpu.VMEM((2 * n, 8, 128), F32),
            pltpu.VMEM((all_rows, cols), BF16),
            pltpu.VMEM((2, n * rows, cols), BF16),
            pltpu.VMEM((all_rows, HD), F32),
            pltpu.VMEM((rows, width), BF16),
            pltpu.VMEM((2 * n, 8, 128), F32),
            pltpu.VMEM((2 * n, 8, 128), F32),
            dma((4 * pieces,)),
            dma((2 * n,)),
            dma((2 * n,)),
            dma((n,)),
            dma((n,)),
            dma((n,)),
            dma((n,)),
            dma((n,)),
            regular,
            regular,
            dma((heads,)),
            dma((heads,)),
            dma((heads,)),
            dma((2 * n,)),
            dma((2 * n,)),
            dma((n,)),
            dma((n,)),
            dma(()),
        ],
        compiler_params=pltpu.CompilerParams(
            collective_id=0, has_side_effects=True, vmem_limit_bytes=VMEM_LIMIT
        ),
        name="layer",
    )(x, norm_gain.reshape(1, width), w, sub_gain.reshape(1, head_cols), w_out)
    return out[None]


def solution(mesh):
    return jax.shard_map(
        functools.partial(body, mesh.shape["tp"]),
        mesh=mesh,
        in_specs=(P("dp", ("ctx", "tp"), None), P(), P(None, None, "tp"), P("tp"), P("tp", None)),
        out_specs=P("dp", ("ctx", "tp"), None),
        check_vma=False,
    )
```
